256 devices in a mesh: row: 32 (over z_lo, x, core), col: 8 (over y, z_hi).
Axes of the slice: x: 4, y: 4, z: 8 (z_hi: 2, z_lo: 4; z = z_hi * 4 + z_lo), core: 2. Of those that a mesh axis runs over, the one named last changes fastest.
Arguments:
- occ_coef: bfloat16 [24576, 4096], P(('row', 'col')), may hold values from -0.25 to 0.25
- vir_coef: bfloat16 [24576, 10240], P(('row', 'col')), may hold values from -0.15811388 to 0.15811388
- occ_weight: float32 [4096], replicated, may hold values from 0.05 to 1
- vir_weight: float32 [10240], replicated, may hold values from 0.02 to 1
- three_center: bfloat16 [2048, 128, 256], P(('row', 'col')), may hold values from -0.59765625 to 0.59765625
- pair_blocks: int32 [2048, 3], P(('row', 'col')), may hold values from 0 to 1535, as said below
- send_pairs: int32 [8192, 1], P(('row', 'col')), may hold values from 0 to 7, as said below
- partners: int32 [2048, 12], P(('row', 'col')), may hold values from 0 to 31, as said below
- partner_blocks: int32 [2048, 12, 3], P(('row', 'col')), may hold values from 0 to 1535, as said below
Outputs:
- chi_slab: float32 [512, 512], P('row', 'col')
The draws below stay inside these ranges and needn't reach their ends.
Inputs may be any that keep to these rules, and one draw needn't show every extreme that they name: pair_blocks[j, 0] and pair_blocks[j, 1] lie in [d * 6, (d + 1) * 6) with d = j // 8; pair_blocks[j, 2] is below 4. `send_pairs`: local pair indices. `partners`: every slot is named by some pair of each device. partner_blocks[j, t] equals pair_blocks[partner[j, t]].
All inputs are finite; a program needn't handle non-finite values.
Results may differ from the reference program's by a relative error of at most 0.0045.
Values may be sent and summed in bfloat16 or wider, within the bound.
No kernel may reach another device: no remote copies, remote signals or barrier semaphores. Data moves between devices by JAX's collectives and lax.ppermute only.
A program may use at most 128 MiB of HBM per device.

```python
import math
import jax
import jax.numpy as jnp
from jax import lax

BB = 16
AB = 128
NOCC = 4096
NVIR = 10240
NBLK = 1536
PAIR_DEV = 8
NNB = 12
CAP = 1
NAB = 4
NPAIR = 2048
N_ROW = 32
N_COL = 8


def layout(key):
    pair_total = PAIR_DEV * N_ROW * N_COL
    device_total = N_ROW * N_COL
    blocks_each = NBLK // device_total
    key_occ, key_vir, key_aux, key_send, key_slot = jax.random.split(jax.random.fold_in(key, 7), 5)
    owner_dev = jnp.arange(pair_total, dtype=jnp.int32) // PAIR_DEV
    owner_row = owner_dev // N_COL
    occ_block = owner_dev * blocks_each + jax.random.randint(key_occ, (pair_total,), 0, blocks_each)
    vir_block = owner_dev * blocks_each + jax.random.randint(key_vir, (pair_total,), 0, blocks_each)
    aux_block = jax.random.randint(key_aux, (pair_total,), 0, NAB)
    block_ids = jnp.stack([occ_block, vir_block, aux_block], axis=1).astype(jnp.int32)
    send_lists = jax.random.randint(key_send, (device_total * N_ROW, CAP), 0, PAIR_DEV).astype(jnp.int32)
    slot_width = PAIR_DEV * NNB
    shuffled = jax.vmap(lambda device_key: jax.random.permutation(device_key, slot_width))(jax.random.split(key_slot, device_total))
    slot_ids = (shuffled % (N_ROW * CAP)).reshape(pair_total, NNB).astype(jnp.int32)
    source_row = slot_ids // CAP
    source_slot = slot_ids % CAP
    source_dev = source_row * N_COL + (owner_dev % N_COL)[:, None]
    partner = source_dev * PAIR_DEV + send_lists[source_dev * N_ROW + owner_row[:, None], source_slot]
    far_ids = block_ids[partner]
    return (block_ids, send_lists, slot_ids, far_ids)


def draw_pair_blocks(key, part):
    return layout(key)[0]


def draw_send_pairs(key, part):
    return layout(key)[1]


def draw_partners(key, part):
    return layout(key)[2]


def draw_partner_blocks(key, part):
    return layout(key)[3]


def smoothed(values):
    return values + 0.4 * (jnp.roll(values, 1, axis=-2) + jnp.roll(values, -1, axis=-2))


def coefficients(key, orbital_count, salt):
    key_base, key_shared = jax.random.split(jax.random.fold_in(key, salt), 2)
    edge_value = math.sqrt(3.0)
    own_part = jax.random.uniform(key_base, (NBLK, BB, orbital_count), jnp.float32, -edge_value, edge_value)
    shared_part = jax.random.uniform(key_shared, (BB, orbital_count), jnp.float32, -edge_value, edge_value)
    values = smoothed(own_part) + 0.8 * smoothed(shared_part)[None]
    return (values / math.sqrt(orbital_count)).reshape(NBLK * BB, orbital_count).astype(jnp.bfloat16)


def draw_occ_coef(key, part):
    return coefficients(key, NOCC, 11)


def draw_vir_coef(key, part):
    return coefficients(key, NVIR, 13)


def shard_levels(stream_key, dims, shards, low, top_value):
    level, own = 1.0, jax.random.fold_in(stream_key, 6)
    for dim, blocks in shards:
        steps = jnp.exp(jax.random.uniform(jax.random.fold_in(own, dim), (blocks,), jnp.float32, low / len(shards), top_value / len(shards)))
        level = level * jnp.repeat(steps, dims[dim] // blocks).reshape([-1 if axis == dim else 1 for axis in range(len(dims))])
    return level


def bell_draw(stream_key, shape, scale, reach, shards=(), kind=jnp.bfloat16):
    result = jax.random.normal(stream_key, shape, jnp.float32) * scale
    if len(shards) > 0:
        result = shard_levels(stream_key, shape, shards, -0.22, 0.18) * result
    return jnp.clip(result, min=-reach, max=reach).astype(kind)


def setup_inputs(seed: int = 0) -> dict:
    streams_of = jax.random.split(jax.random.key(seed), 10)
    occ_coef = draw_occ_coef(jax.random.fold_in(streams_of[9], 71), 0)
    vir_coef = draw_vir_coef(jax.random.fold_in(streams_of[9], 71), 0)
    occ_weight = jnp.clip(jnp.exp(jax.random.uniform(streams_of[2], (NOCC,), jnp.float32, math.log(0.05), math.log(1.0))), 0.05, 1.0)
    vir_weight = jnp.clip(jnp.exp(jax.random.uniform(streams_of[3], (NVIR,), jnp.float32, math.log(0.02), math.log(1.0))), 0.02, 1.0)
    three_center = bell_draw(streams_of[4], (NPAIR, AB, BB * BB), 0.1, 0.59765625, ((0, 256),))
    pair_blocks = draw_pair_blocks(jax.random.fold_in(streams_of[9], 71), 0)
    send_pairs = draw_send_pairs(jax.random.fold_in(streams_of[9], 71), 0)
    partners = draw_partners(jax.random.fold_in(streams_of[9], 71), 0)
    partner_blocks = draw_partner_blocks(jax.random.fold_in(streams_of[9], 71), 0)
    return dict(occ_coef=occ_coef, vir_coef=vir_coef, occ_weight=occ_weight, vir_weight=vir_weight, three_center=three_center, pair_blocks=pair_blocks, send_pairs=send_pairs, partners=partners, partner_blocks=partner_blocks)


def partner_index(pair_blocks, send_pairs, partners):
    pair_total = pair_blocks.shape[0]
    owner_dev = jnp.arange(pair_total, dtype=jnp.int32) // PAIR_DEV
    owner_row = owner_dev // N_COL
    owner_col = owner_dev % N_COL
    source_row = partners // CAP
    source_slot = partners % CAP
    source_dev = source_row * N_COL + owner_col[:, None]
    picked = send_pairs[source_dev * N_ROW + owner_row[:, None], source_slot]
    return (source_dev * PAIR_DEV + picked).astype(jnp.int32)


def reference(occ_coef, vir_coef, occ_weight, vir_weight, three_center, pair_blocks, send_pairs, partners, partner_blocks):
    scaled_occ = (occ_coef.astype(jnp.float32) * occ_weight[None, :]).astype(jnp.bfloat16).reshape(NBLK, BB, NOCC)
    scaled_vir = (vir_coef.astype(jnp.float32) * vir_weight[None, :]).astype(jnp.bfloat16).reshape(NBLK, BB, NVIR)
    occ_blocks = occ_coef.reshape(NBLK, BB, NOCC)
    vir_blocks = vir_coef.reshape(NBLK, BB, NVIR)
    partner = partner_index(pair_blocks, send_pairs, partners)
    group_size = PAIR_DEV
    turn_count = pair_blocks.shape[0] // group_size
    aux_total = NAB * AB
    inputs = (three_center.reshape(turn_count, group_size, AB, BB * BB),
              pair_blocks.reshape(turn_count, group_size, 3),
              partner.reshape(turn_count, group_size, NNB),
              partner_blocks.reshape(turn_count, group_size, NNB, 3))

    def device_terms(chi_acc, pieces):
        own_blocks, own_ids, far_pairs, far_ids = pieces
        blocks_split = three_center[far_pairs].astype(jnp.float32).reshape(group_size, NNB, AB, BB, BB)
        own_occ = scaled_occ[own_ids[:, 0]].astype(jnp.float32)
        far_occ = occ_blocks[far_ids[:, :, 0]].astype(jnp.float32)
        occ_tiles = jnp.einsum("gmi,gtli->gtml", own_occ, far_occ, precision=lax.Precision.HIGHEST).astype(jnp.bfloat16).astype(jnp.float32)
        own_vir = scaled_vir[own_ids[:, 1]].astype(jnp.float32)
        far_vir = vir_blocks[far_ids[:, :, 1]].astype(jnp.float32)
        vir_tiles = jnp.einsum("gna,gtsa->gtns", own_vir, far_vir, precision=lax.Precision.HIGHEST).astype(jnp.bfloat16).astype(jnp.float32)
        mixed_occ = jnp.einsum("gtml,gtqls->gtqms", occ_tiles, blocks_split).astype(jnp.bfloat16)
        paired = jnp.einsum("gtns,gtqms->gtqmn", vir_tiles, mixed_occ.astype(jnp.float32)).astype(jnp.bfloat16)
        chi_tiles = jnp.einsum("gpk,gtqk->gtpq", own_blocks.astype(jnp.float32),
                               paired.astype(jnp.float32).reshape(group_size, NNB, AB, BB * BB))
        far_hot = (far_ids[:, :, 2][:, :, None] == jnp.arange(NAB, dtype=jnp.int32)).astype(jnp.float32)
        tile_rows = jnp.einsum("gtpq,gtb->gpbq", chi_tiles, far_hot).reshape(group_size, AB, aux_total)
        own_hot = (own_ids[:, 2][:, None] == jnp.arange(NAB, dtype=jnp.int32)).astype(jnp.float32)
        return chi_acc + jnp.einsum("gb,gpc->bpc", own_hot, tile_rows), None

    start_value = jnp.zeros((NAB, AB, aux_total), jnp.float32)
    chi_acc, unused = lax.scan(device_terms, start_value, inputs)
    return chi_acc.reshape(aux_total, aux_total)
```

```python
import functools

import jax
import jax.numpy as jnp
from jax import lax
from jax.experimental import pallas as pl
from jax.experimental.pallas import tpu as pltpu
from jax.sharding import Mesh, PartitionSpec as P

BB = 16
AB = 128
NNB = 12
NAB = 4
NJ = 8
NZ = 4
NX = 4
NS = NZ * NX
LOCAL = 6
KO = 256
KV = 640
KS = KO + KV
ROWS = LOCAL * BB
TR = NNB * BB
ALL = ("zl", "x", "c", "y", "zh")
f32 = jnp.float32
bf16 = jnp.bfloat16


def dens_kernel(tab, pos, mine, other, wts, out0, out1, out2, out3, own, far, prod):
    zl, x, c = pos[0], pos[1], pos[2]
    lane = lax.broadcasted_iota(jnp.int32, (BB, NJ * BB), 1) // BB
    w_occ = wts[0:1, 0:KO]
    w_vir = wts[0:1, KO:KS]
    for k, out in enumerate((out0, out1, out2, out3)):

        def per_dest(m, carry, k=k, out=out):
            d = ((zl + m) % NZ) * NX + (x + k) % NX
            at_row = m * NX + k
            for j in range(NJ):
                a = pl.multiple_of(tab[at_row, 64 + j] * BB, BB)
                b = pl.multiple_of(tab[at_row, 72 + j] * BB, BB)
                rows = slice(j * BB, (j + 1) * BB)
                own[rows, 0:KO] = (mine[d, pl.ds(a, BB), 0:KO].astype(f32) * w_occ).astype(bf16)
                own[rows, KO:KS] = (mine[d, pl.ds(b, BB), KO:KS].astype(f32) * w_vir).astype(bf16)
            for p in range(NS):
                for q, src in enumerate((mine, other)):
                    e = 2 * p + (c ^ q)
                    a = pl.multiple_of(tab[at_row, e] * BB, BB)
                    b = pl.multiple_of(tab[at_row, 32 + e] * BB, BB)
                    to = pl.ds(pl.multiple_of(e * BB, BB), BB)
                    far[to, 0:KO] = src[p, pl.ds(a, BB), 0:KO]
                    far[to, KO:KS] = src[p, pl.ds(b, BB), KO:KS]
            dims = (((1,), (1,)), ((), ()))
            prod[0] = lax.dot_general(far[:, 0:KO], own[:, 0:KO], dims, preferred_element_type=f32)
            prod[1] = lax.dot_general(far[:, KO:KS], own[:, KO:KS], dims, preferred_element_type=f32)
            for t in range(NNB):
                parts = [None, None]
                for j in range(NJ):
                    at = pl.multiple_of(tab[at_row, 128 + j * NNB + t] * BB, BB)
                    for kind in range(2):
                        row = prod[kind, pl.ds(at, BB), :]
                        parts[kind] = row if j == 0 else jnp.where(lane == j, row, parts[kind])
                for kind in range(2):
                    out[m, kind * TR + t * BB : kind * TR + (t + 1) * BB, :] = parts[kind].astype(bf16)
            return carry

        lax.fori_loop(0, NZ, per_dest, 0)


def tile_kernel(meta, t0, t1, t2, t3, recv, own, out, dens, occ_exp, vir_exp, kron, acc, chi):
    total = t0[...].astype(f32) + t1[...].astype(f32) + t2[...].astype(f32) + t3[...].astype(f32)
    dens[...] = total.astype(bf16)
    chi[...] = jnp.zeros_like(chi)
    row = lax.broadcasted_iota(jnp.int32, (NJ * BB, BB * BB), 0)
    col = lax.broadcasted_iota(jnp.int32, (NJ * BB, BB * BB), 1)

    def per_pair(j, carry):
        hot_occ = (row == j * BB + col // BB).astype(f32).astype(bf16)
        hot_vir = (row == j * BB + col % BB).astype(f32).astype(bf16)
        occ_exp[...] = jnp.dot(dens[0:TR, :], hot_occ, preferred_element_type=f32)
        vir_exp[...] = jnp.dot(dens[TR : 2 * TR, :], hot_vir, preferred_element_type=f32)
        acc[...] = jnp.zeros_like(acc)
        for t in range(NNB):
            buf = t % 2
            vir = vir_exp[t * BB : (t + 1) * BB, :]
            for lam in range(BB):
                occ = jnp.broadcast_to(occ_exp[t * BB + lam : t * BB + lam + 1, :], (BB, BB * BB))
                kron[buf, lam * BB : (lam + 1) * BB, :] = (occ * vir).astype(bf16)
            slot = meta[j * NNB + t]
            aux = meta[128 + j * NNB + t]
            paired = jnp.dot(recv[slot], kron[buf], preferred_element_type=f32)
            acc[aux] = acc[aux] + paired
        target = meta[240 + j]
        rows = acc[...].reshape(NAB * AB, BB * BB).astype(bf16)
        chi[target] += lax.dot_general(
            own[j], rows, (((1,), (1,)), ((), ())), preferred_element_type=f32
        )
        return carry

    lax.fori_loop(0, NJ, per_pair, 0)
    low = lax.broadcasted_iota(jnp.int32, (1, 8, 128), 2) < 64
    for tile in range(4):
        grid = chi[:, :, tile * 128 : (tile + 1) * 128].reshape(32, 2, 8, 128)
        top, bot = grid[:, 0], grid[:, 1]
        even = jnp.where(low, top, pltpu.roll(bot, 64, 2))
        odd = jnp.where(low, pltpu.roll(top, 64, 2), bot)
        out[:, 2 * tile] = even.astype(bf16)
        out[:, 2 * tile + 1] = odd.astype(bf16)


def around(rows, axis, size):
    parts = [rows]
    for k in range(1, size):
        parts.append(lax.ppermute(rows, axis, [((i + k) % size, i) for i in range(size)]))
    return jnp.concatenate(parts, axis=0)


def body(
    occ_coef,
    vir_coef,
    occ_weight,
    vir_weight,
    three_center,
    pair_blocks,
    send_pairs,
    partners,
    partner_blocks,
):
    zl, x, c = lax.axis_index("zl"), lax.axis_index("x"), lax.axis_index("c")
    share = zl * NX + x
    payload = jnp.concatenate(
        [
            occ_coef.reshape(ROWS, NS, KO).transpose(1, 0, 2),
            vir_coef.reshape(ROWS, NS, KV).transpose(1, 0, 2),
        ],
        axis=2,
    )
    mine = lax.all_to_all(payload, ("zl", "x"), split_axis=0, concat_axis=0, tiled=True)

    wts = jnp.concatenate(
        [
            lax.dynamic_slice_in_dim(occ_weight, share * KO, KO),
            lax.dynamic_slice_in_dim(vir_weight, share * KV, KV),
        ]
    ).reshape(1, KS)
    slots = partners.reshape(-1)
    far_ids = partner_blocks.reshape(-1, 3)
    own_local = pair_blocks % LOCAL
    far_local = far_ids % LOCAL
    hot = slots[:, None] == jnp.arange(32, dtype=jnp.int32)[None, :]
    slot_occ = jnp.max(jnp.where(hot, far_local[:, 0:1], 0), axis=0)
    slot_vir = jnp.max(jnp.where(hot, far_local[:, 1:2], 0), axis=0)
    pad = jnp.zeros((48,), jnp.int32)
    table = jnp.concatenate(
        [slot_occ, slot_vir, own_local[:, 0], own_local[:, 1], pad, slots, pad[:32]]
    )
    tables = around(around(table.reshape(1, 256), "x", NX), "zl", NZ)
    pos = jnp.stack([zl, x, c, share]).astype(jnp.int32)
    out_blocks = three_center[send_pairs.reshape(-1)]

    mine, out_blocks, tables, wts = lax.optimization_barrier((mine, out_blocks, tables, wts))
    received = lax.all_to_all(
        out_blocks, ("zl", "x", "c"), split_axis=0, concat_axis=0, tiled=True
    )
    other = lax.ppermute(mine, "c", [(0, 1), (1, 0)])

    vmem = pl.BlockSpec(memory_space=pltpu.VMEM)
    smem = pl.BlockSpec(memory_space=pltpu.SMEM)
    part = jax.ShapeDtypeStruct((NZ, 2 * TR, NJ * BB), bf16)
    partials = pl.pallas_call(
        dens_kernel,
        out_shape=(part,) * NX,
        in_specs=[smem, smem, vmem, vmem, vmem],
        out_specs=(vmem,) * NX,
        scratch_shapes=[
            pltpu.VMEM((NJ * BB, KS), bf16),
            pltpu.VMEM((32 * BB, KS), bf16),
            pltpu.VMEM((2, 32 * BB, NJ * BB), f32),
        ],
        compiler_params=pltpu.CompilerParams(vmem_limit_bytes=32 << 20),
        cost_estimate=pl.CostEstimate(
            flops=2 * NS * 512 * 128 * KS, bytes_accessed=8 << 20, transcendentals=0
        ),
        name="density_partials",
    )(tables, pos, mine, other, wts)
    summed = partials[0].astype(f32)
    for k in range(1, NX):
        moved = lax.ppermute(partials[k], "x", [(i, (i + k) % NX) for i in range(NX)])
        summed = summed + moved.astype(f32)
    tiles = [summed[0].astype(bf16)]
    for m in range(1, NZ):
        tiles.append(
            lax.ppermute(summed[m].astype(bf16), "zl", [(i, (i + m) % NZ) for i in range(NZ)])
        )

    pad32 = pad[:32]
    meta = jnp.concatenate([slots, pad32, far_ids[:, 2], pad[:16], pair_blocks[:, 2], pad[:8]])
    packed = pl.pallas_call(
        tile_kernel,
        out_shape=jax.ShapeDtypeStruct((32, 8, 8, 128), bf16),
        in_specs=[smem] + [vmem] * 6,
        out_specs=vmem,
        scratch_shapes=[
            pltpu.VMEM((2 * TR, NJ * BB), bf16),
            pltpu.VMEM((TR, BB * BB), f32),
            pltpu.VMEM((TR, BB * BB), f32),
            pltpu.VMEM((2, BB * BB, BB * BB), bf16),
            pltpu.VMEM((NAB, AB, BB * BB), f32),
            pltpu.VMEM((NAB, AB, NAB * AB), f32),
        ],
        compiler_params=pltpu.CompilerParams(vmem_limit_bytes=32 << 20),
        cost_estimate=pl.CostEstimate(
            flops=2 * 96 * 128 * 256 * 256, bytes_accessed=4 << 20, transcendentals=0
        ),
        name="chi_tiles",
    )(meta, *tiles, received, three_center)

    gathered = lax.all_to_all(
        packed.reshape(256, 8, 128), ALL, split_axis=0, concat_axis=0, tiled=True
    )
    total = jnp.sum(gathered.astype(f32), axis=0)
    return jnp.concatenate([total[:, :64], total[:, 64:]], axis=0)


def solution(mesh):
    fine = Mesh(mesh.devices.reshape(4, 4, 2, 4, 2), ALL)
    return jax.shard_map(
        body,
        mesh=fine,
        in_specs=(
            P(ALL, None),
            P(ALL, None),
            P(),
            P(),
            P(ALL, None, None),
            P(ALL, None),
            P(ALL, None),
            P(ALL, None),
            P(ALL, None, None),
        ),
        out_specs=P(("zl", "x", "c"), ("y", "zh")),
        check_vma=False,
    )
```

```python
import functools

import jax
import jax.numpy as jnp
from jax import lax
from jax.experimental import pallas as pl
from jax.experimental.pallas import tpu as pltpu
from jax.sharding import Mesh, PartitionSpec as P

BB = 16
AB = 128
NNB = 12
NAB = 4
NJ = 8
NZ = 4
NX = 4
NS = NZ * NX
LOCAL = 6
KO = 256
KV = 640
ROWS = LOCAL * BB
TR = NNB * BB
LANES = 128
TO = KO // LANES
TV = KV // LANES
KT = TO + TV
BLK = KT * BB
PAY = LOCAL * BLK + 8
ALL = ("zl", "x", "c", "y", "zh")
f32 = jnp.float32
bf16 = jnp.bfloat16


def table_of(ids, slots, far_ids):
    lane = lax.broadcasted_iota(jnp.int32, (NJ, LANES), 1)
    diag = lax.broadcasted_iota(jnp.int32, (NJ, NJ), 0) == lax.broadcasted_iota(jnp.int32, (NJ, NJ), 1)
    slot = slots[...]

    def local(block):
        return block - LOCAL * jnp.floor((block.astype(f32) + 0.5) * (1.0 / LOCAL)).astype(jnp.int32)

    own = local(ids[...])
    far_occ, far_vir = local(far_ids[0]), local(far_ids[1])
    rows = jnp.zeros((NJ, LANES), jnp.int32)
    for kind in range(2):
        column = jnp.sum(jnp.where(diag, own[kind : kind + 1, :], 0), axis=1, keepdims=True)
        rows = jnp.where(lane == 16 + kind, column, rows)
    seen = jnp.zeros((NJ, LANES), jnp.int32)
    for t in range(NNB):
        here = slot[:, t : t + 1]
        rows = jnp.where(lane == t, here, rows)
        seen = jnp.where(lane == here + 32, jnp.maximum(seen, far_occ[:, t : t + 1]), seen)
        seen = jnp.where(lane == here + 64, jnp.maximum(seen, far_vir[:, t : t + 1]), seen)
    rows = rows + jnp.max(seen, axis=0, keepdims=True)
    return rows.astype(f32).astype(bf16)


def payload_kernel(occ, vir, *refs):
    given, (out, occ_in, vir_in, packed, *small, sems_in, sems_out) = refs[:3], refs[3:]
    copies = [pltpu.make_async_copy(given[n], small[n], sems_in.at[NS, n]) for n in range(3)]
    for copy in copies:
        copy.start()
    loads, stores = [], []
    for s in range(NS):
        loads.append(
            (
                pltpu.make_async_copy(occ.at[:, pl.ds(s * KO, KO)], occ_in.at[s], sems_in.at[s, 0]),
                pltpu.make_async_copy(vir.at[:, pl.ds(s * KV, KV)], vir_in.at[s], sems_in.at[s, 1]),
            )
        )
        for load in loads[-1]:
            load.start()
    for copy in copies:
        copy.wait()
    table = table_of(*small)
    for s in range(NS):
        for load in loads[s]:
            load.wait()
        for blk in range(LOCAL):
            rows = slice(blk * BB, (blk + 1) * BB)
            for kt in range(KT):
                at = blk * BLK + kt * BB
                stage, first = (occ_in, kt) if kt < TO else (vir_in, kt - TO)
                packed[s, at : at + BB, :] = stage[s, rows, first * LANES : (first + 1) * LANES]
        packed[s, LOCAL * BLK : PAY, :] = table
        stores.append(pltpu.make_async_copy(packed.at[s], out.at[s], sems_out.at[s]))
        stores[-1].start()
    for store in stores:
        store.wait()


def payload_call(occ_coef, vir_coef, extra):
    hbm = pl.BlockSpec(memory_space=pltpu.HBM)
    return pl.pallas_call(
        payload_kernel,
        out_shape=jax.ShapeDtypeStruct((NS, PAY, LANES), bf16),
        in_specs=[hbm] * 5,
        out_specs=hbm,
        scratch_shapes=[
            pltpu.VMEM((NS, ROWS, KO), bf16),
            pltpu.VMEM((NS, ROWS, KV), bf16),
            pltpu.VMEM((NS, PAY, LANES), bf16),
        ]
        + [pltpu.VMEM(part.shape, part.dtype) for part in extra]
        + [pltpu.SemaphoreType.DMA((NS + 1, 3)), pltpu.SemaphoreType.DMA((NS,))],
        compiler_params=pltpu.CompilerParams(vmem_limit_bytes=60 << 20),
        cost_estimate=pl.CostEstimate(flops=0, bytes_accessed=6 << 20, transcendentals=0),
        name="coef_payload",
    )(occ_coef, vir_coef, *extra)


def tile_of(parts, kt):
    return parts[0][kt * BB : (kt + 1) * BB] if kt < TO else parts[1][(kt - TO) * BB : (kt - TO + 1) * BB]


def dens_kernel(jobs, tab, pos, mine, other, wts, *refs):
    outs, (own, far, prod) = refs[: len(jobs)], refs[len(jobs) :]
    zl, x, c = pos[0], pos[1], pos[2]
    lane = lax.broadcasted_iota(jnp.int32, (BB, NJ * BB), 1) // BB
    dims = (((1,), (1,)), ((), ()))
    for (k, start, count), out in zip(jobs, outs):

        def per_dest(m, carry, k=k, start=start, out=out):
            d = ((zl + start + m) % NZ) * NX + (x + k) % NX
            base = d * 8
            for j in range(NJ):
                a = pl.multiple_of(tab[base + j, 16] * BLK, BB)
                b = pl.multiple_of(tab[base + j, 17] * BLK + TO * BB, BB)
                parts = (mine[d, pl.ds(a, TO * BB), :], mine[d, pl.ds(b, TV * BB), :])
                for kt in range(KT):
                    block = tile_of(parts, kt).astype(f32) * wts[kt : kt + 1, :]
                    own[j * BB : (j + 1) * BB, kt * LANES : (kt + 1) * LANES] = block.astype(bf16)
            for p in range(NS):
                for q, src in enumerate((mine, other)):
                    e = 2 * p + (c ^ q)
                    a = pl.multiple_of(tab[base, 32 + e] * BLK, BB)
                    b = pl.multiple_of(tab[base, 64 + e] * BLK + TO * BB, BB)
                    to = pl.ds(pl.multiple_of(e * BB, BB), BB)
                    parts = (src[p, pl.ds(a, TO * BB), :], src[p, pl.ds(b, TV * BB), :])
                    for kt in range(KT):
                        far[to, kt * LANES : (kt + 1) * LANES] = tile_of(parts, kt)
            for kind, cols in enumerate((slice(0, KO), slice(KO, KO + KV))):
                prod[kind] = lax.dot_general(
                    far[:, cols], own[:, cols], dims, preferred_element_type=f32
                ).astype(bf16)
            for t in range(NNB):
                picked = [None, None]
                for j in range(NJ):
                    at = pl.multiple_of(tab[base + j, t] * BB, BB)
                    for kind in range(2):
                        row = prod[kind, pl.ds(at, BB), :]
                        picked[kind] = row if j == 0 else jnp.where(lane == j, row, picked[kind])
                for kind in range(2):
                    out[m, kind * TR + t * BB : kind * TR + (t + 1) * BB, :] = picked[kind]
            return carry

        lax.fori_loop(0, count, per_dest, 0)


def dens_call(jobs, tables, pos, mine, other, wts):
    vmem = pl.BlockSpec(memory_space=pltpu.VMEM)
    smem = pl.BlockSpec(memory_space=pltpu.SMEM)
    parts = tuple(jax.ShapeDtypeStruct((job[2], 2 * TR, NJ * BB), bf16) for job in jobs)
    return pl.pallas_call(
        functools.partial(dens_kernel, jobs),
        out_shape=parts,
        in_specs=[smem, smem, vmem, vmem, vmem],
        out_specs=(vmem,) * len(jobs),
        scratch_shapes=[
            pltpu.VMEM((NJ * BB, KO + KV), bf16),
            pltpu.VMEM((32 * BB, KO + KV), bf16),
            pltpu.VMEM((2, 32 * BB, NJ * BB), bf16),
        ],
        compiler_params=pltpu.CompilerParams(vmem_limit_bytes=24 << 20),
        cost_estimate=pl.CostEstimate(
            flops=2 * sum(job[2] for job in jobs) * 512 * 128 * (KO + KV), bytes_accessed=6 << 20, transcendentals=0
        ),
        name="density_partials",
    )(tables, pos, mine, other, wts)


def tile_kernel(
    meta, t0, t1, t2, t3, blocks, own, keep, give, recv, dens, occ_exp, vir_exp, kron, acc, chi, sem
):
    load = pltpu.make_async_copy(blocks, recv, sem)
    load.start()
    total = t0[...].astype(f32) + t1[...].astype(f32) + t2[...].astype(f32) + t3[...].astype(f32)
    dens[...] = total.astype(bf16)
    chi[...] = jnp.zeros_like(chi)
    row = lax.broadcasted_iota(jnp.int32, (NJ * BB, BB * BB), 0)
    col = lax.broadcasted_iota(jnp.int32, (NJ * BB, BB * BB), 1)

    load.wait()

    def per_pair(j, carry):
        hot_occ = (row == j * BB + col // BB).astype(f32).astype(bf16)
        hot_vir = (row == j * BB + col % BB).astype(f32).astype(bf16)
        occ_exp[...] = jnp.dot(dens[0:TR, :], hot_occ, preferred_element_type=f32)
        vir_exp[...] = jnp.dot(dens[TR : 2 * TR, :], hot_vir, preferred_element_type=f32)
        acc[...] = jnp.zeros_like(acc)
        for t in range(NNB):
            buf = t % 2
            vir = vir_exp[t * BB : (t + 1) * BB, :]
            for lam in range(BB):
                occ = jnp.broadcast_to(occ_exp[t * BB + lam : t * BB + lam + 1, :], (BB, BB * BB))
                kron[buf, lam * BB : (lam + 1) * BB, :] = (occ * vir).astype(bf16)
            slot = meta[j * NNB + t]
            aux = meta[128 + j * NNB + t]
            paired = jnp.dot(recv[slot], kron[buf], preferred_element_type=f32)
            acc[aux] = acc[aux] + paired
        target = meta[240 + j]
        rows = acc[...].reshape(NAB * AB, BB * BB).astype(bf16)
        chi[target] += lax.dot_general(
            own[j], rows, (((1,), (1,)), ((), ())), preferred_element_type=f32
        )
        return carry

    lax.fori_loop(0, NJ, per_pair, 0)
    low = lax.broadcasted_iota(jnp.int32, (1, 8, 128), 2) < 64
    first = jnp.full((1, 8, 128), meta[248], jnp.int32) == 0
    for tile in range(4):
        grid = chi[:, :, tile * 128 : (tile + 1) * 128].reshape(NS, 2, 2, 8, 128)
        for side, col in enumerate((2 * tile, 2 * tile + 1)):
            packed = []
            for core in range(2):
                top, bot = grid[:, core, 0], grid[:, core, 1]
                if side == 0:
                    packed.append(jnp.where(low, top, pltpu.roll(bot, 64, 2)))
                else:
                    packed.append(jnp.where(low, pltpu.roll(top, 64, 2), bot))
            keep[:, col] = jnp.where(first, packed[0], packed[1])
            give[:, col] = jnp.where(first, packed[1], packed[0])


def shift(rows, axis, size, k):
    return lax.ppermute(rows, axis, [(i, (i + k) % size) for i in range(size)]) if k else rows


def body(
    occ_coef,
    vir_coef,
    occ_weight,
    vir_weight,
    three_center,
    pair_blocks,
    send_pairs,
    partners,
    partner_blocks,
):
    zl, x, c = lax.axis_index("zl"), lax.axis_index("x"), lax.axis_index("c")
    share = zl * NX + x
    vmem = pl.BlockSpec(memory_space=pltpu.VMEM)
    smem = pl.BlockSpec(memory_space=pltpu.SMEM)
    whole = pl.BlockSpec(memory_space=pl.ANY)
    spread_out = functools.partial(lax.all_to_all, split_axis=0, concat_axis=0, tiled=True)
    extra = (pair_blocks.T, partners, partner_blocks.transpose(2, 0, 1))
    mine = spread_out(payload_call(occ_coef, vir_coef, extra), ("zl", "x"))
    out_blocks = three_center[send_pairs.reshape(-1)]
    wts = jnp.concatenate(
        [
            lax.dynamic_slice_in_dim(occ_weight, share * KO, KO),
            lax.dynamic_slice_in_dim(vir_weight, share * KV, KV),
        ]
    ).reshape(KT, LANES)
    pos = jnp.stack([zl, x, c, share]).astype(jnp.int32)
    mine, out_blocks, wts, pos = lax.optimization_barrier((mine, out_blocks, wts, pos))
    received = spread_out(out_blocks, ("zl", "x", "c"))
    swap = [(0, 1), (1, 0)]
    tables = mine[:, LOCAL * BLK :, :].astype(jnp.int32).reshape(NS * 8, LANES)
    other = lax.ppermute(mine, "c", swap)
    ahead, behind = dens_call(((2, 0, 2), (2, 2, 2)), tables, pos, mine, other, wts)
    ahead, behind = shift(ahead, "x", NX, 1), shift(behind, "x", NX, NX - 1)
    part1, part3, part0 = dens_call(
        ((1, 0, NZ), (3, 0, NZ), (0, 0, NZ)), tables, pos, mine, other, wts
    )
    part1 = jnp.concatenate([(part1[:2].astype(f32) + ahead.astype(f32)).astype(bf16), part1[2:]])
    part3 = jnp.concatenate([part3[:2], (part3[2:].astype(f32) + behind.astype(f32)).astype(bf16)])
    summed = part0.astype(f32)
    summed = summed + shift(part1, "x", NX, 1).astype(f32)
    summed = summed + shift(part3, "x", NX, NX - 1).astype(f32)
    tiles = [shift(summed[m].astype(bf16), "zl", NZ, m) for m in range(NZ)]

    slots = partners.reshape(-1)
    pad = jnp.zeros((32,), jnp.int32)
    far_aux = partner_blocks[:, :, 2].reshape(-1)
    meta = jnp.concatenate(
        [slots, pad, far_aux, pad[:16], pair_blocks[:, 2], c.astype(jnp.int32)[None], pad[:7]]
    )
    half = jax.ShapeDtypeStruct((NS, 8, 8, 128), f32)
    keep, give = pl.pallas_call(
        tile_kernel,
        out_shape=(half, half),
        in_specs=[smem] + [vmem] * 4 + [whole, vmem],
        out_specs=(vmem, vmem),
        scratch_shapes=[
            pltpu.VMEM((32, AB, BB * BB), bf16),
            pltpu.VMEM((2 * TR, NJ * BB), bf16),
            pltpu.VMEM((TR, BB * BB), f32),
            pltpu.VMEM((TR, BB * BB), f32),
            pltpu.VMEM((2, BB * BB, BB * BB), bf16),
            pltpu.VMEM((NAB, AB, BB * BB), f32),
            pltpu.VMEM((NAB, AB, NAB * AB), f32),
            pltpu.SemaphoreType.DMA,
        ],
        compiler_params=pltpu.CompilerParams(vmem_limit_bytes=32 << 20),
        cost_estimate=pl.CostEstimate(
            flops=2 * 96 * 128 * 256 * 256, bytes_accessed=4 << 20, transcendentals=0
        ),
        name="chi_tiles",
    )(meta, *tiles, received, three_center)

    pair_sum = keep + lax.ppermute(give, "c", swap)
    gathered = lax.all_to_all(
        pair_sum.astype(bf16).reshape(128, 8, 128),
        ("zl", "x", "y", "zh"),
        split_axis=0,
        concat_axis=0,
        tiled=True,
    )
    total = jnp.sum(gathered.astype(f32), axis=0)
    return jnp.concatenate([total[:, :64], total[:, 64:]], axis=0)


def solution(mesh):
    fine = Mesh(mesh.devices.reshape(4, 4, 2, 4, 2), ALL)
    return jax.shard_map(
        body,
        mesh=fine,
        in_specs=(
            P(ALL, None),
            P(ALL, None),
            P(),
            P(),
            P(ALL, None, None),
            P(ALL, None),
            P(ALL, None),
            P(ALL, None),
            P(ALL, None, None),
        ),
        out_specs=P(("zl", "x", "c"), ("y", "zh")),
        check_vma=False,
    )
```

```python
import functools

import jax
import jax.numpy as jnp
from jax import lax
from jax.experimental import pallas as pl
from jax.experimental.pallas import tpu as pltpu
from jax.sharding import Mesh, PartitionSpec as P

BB = 16
AB = 128
NNB = 12
NAB = 4
NJ = 8
NZ = 4
NX = 4
NS = NZ * NX
LOCAL = 6
KO = 256
KV = 640
ROWS = LOCAL * BB
TR = NNB * BB
LANES = 128
TO = KO // LANES
TV = KV // LANES
KT = TO + TV
BLK = KT * BB
PAY = LOCAL * BLK + 8
ZL = ("zb", "za")
ZX = ("zb", "za", "x")
ALL = ("zb", "za", "x", "c", "y", "zh")
f32 = jnp.float32
bf16 = jnp.bfloat16


def table_of(ids, slots, far_ids):
    lane = lax.broadcasted_iota(jnp.int32, (NJ, LANES), 1)
    diag = lax.broadcasted_iota(jnp.int32, (NJ, NJ), 0) == lax.broadcasted_iota(jnp.int32, (NJ, NJ), 1)
    slot = slots[...]

    def local(block):
        return block - LOCAL * jnp.floor((block.astype(f32) + 0.5) * (1.0 / LOCAL)).astype(jnp.int32)

    own = local(ids[...])
    far_occ, far_vir = local(far_ids[0]), local(far_ids[1])
    rows = jnp.zeros((NJ, LANES), jnp.int32)
    for kind in range(2):
        column = jnp.sum(jnp.where(diag, own[kind : kind + 1, :], 0), axis=1, keepdims=True)
        rows = jnp.where(lane == 16 + kind, column, rows)
    seen = jnp.zeros((NJ, LANES), jnp.int32)
    for t in range(NNB):
        here = slot[:, t : t + 1]
        rows = jnp.where(lane == t, here, rows)
        seen = jnp.where(lane == here + 32, jnp.maximum(seen, far_occ[:, t : t + 1]), seen)
        seen = jnp.where(lane == here + 64, jnp.maximum(seen, far_vir[:, t : t + 1]), seen)
    rows = rows + jnp.max(seen, axis=0, keepdims=True)
    return rows.astype(f32).astype(bf16)


def payload_kernel(occ, vir, *refs):
    given, (out, occ_in, vir_in, packed, *small, sems_in, sems_out) = refs[:3], refs[3:]
    copies = [pltpu.make_async_copy(given[n], small[n], sems_in.at[NS, n]) for n in range(3)]
    for copy in copies:
        copy.start()
    loads, stores = [], []
    for s in range(NS):
        loads.append(
            (
                pltpu.make_async_copy(occ.at[:, pl.ds(s * KO, KO)], occ_in.at[s], sems_in.at[s, 0]),
                pltpu.make_async_copy(vir.at[:, pl.ds(s * KV, KV)], vir_in.at[s], sems_in.at[s, 1]),
            )
        )
        for load in loads[-1]:
            load.start()
    for copy in copies:
        copy.wait()
    table = table_of(*small)
    for s in range(NS):
        for load in loads[s]:
            load.wait()
        for blk in range(LOCAL):
            rows = slice(blk * BB, (blk + 1) * BB)
            for kt in range(KT):
                at = blk * BLK + kt * BB
                stage, first = (occ_in, kt) if kt < TO else (vir_in, kt - TO)
                packed[s, at : at + BB, :] = stage[s, rows, first * LANES : (first + 1) * LANES]
        packed[s, LOCAL * BLK : PAY, :] = table
        stores.append(pltpu.make_async_copy(packed.at[s], out.at[s], sems_out.at[s]))
        stores[-1].start()
    for store in stores:
        store.wait()


def payload_call(occ_coef, vir_coef, extra):
    hbm = pl.BlockSpec(memory_space=pltpu.HBM)
    return pl.pallas_call(
        payload_kernel,
        out_shape=jax.ShapeDtypeStruct((NS, PAY, LANES), bf16),
        in_specs=[hbm] * 5,
        out_specs=hbm,
        scratch_shapes=[
            pltpu.VMEM((NS, ROWS, KO), bf16),
            pltpu.VMEM((NS, ROWS, KV), bf16),
            pltpu.VMEM((NS, PAY, LANES), bf16),
        ]
        + [pltpu.VMEM(part.shape, part.dtype) for part in extra]
        + [pltpu.SemaphoreType.DMA((NS + 1, 3)), pltpu.SemaphoreType.DMA((NS,))],
        compiler_params=pltpu.CompilerParams(vmem_limit_bytes=60 << 20),
        cost_estimate=pl.CostEstimate(flops=0, bytes_accessed=6 << 20, transcendentals=0),
        name="coef_payload",
    )(occ_coef, vir_coef, *extra)


def tile_of(parts, kt):
    return parts[0][kt * BB : (kt + 1) * BB] if kt < TO else parts[1][(kt - TO) * BB : (kt - TO + 1) * BB]


def dens_kernel(jobs, tab, pos, mine, other, wts, *refs):
    outs, scratch = refs[: len(jobs)], refs[len(jobs) :]
    zl, x, c = pos[0], pos[1], pos[2]
    lane = lax.broadcasted_iota(jnp.int32, (BB, NJ * BB), 1) // BB
    dims = (((1,), (1,)), ((), ()))

    def gather(d, own, far):
        base = d * 8
        for j in range(NJ):
            a = pl.multiple_of(tab[base + j, 16] * BLK, BB)
            b = pl.multiple_of(tab[base + j, 17] * BLK + TO * BB, BB)
            parts = (mine[d, pl.ds(a, TO * BB), :], mine[d, pl.ds(b, TV * BB), :])
            for kt in range(KT):
                block = tile_of(parts, kt).astype(f32) * wts[kt : kt + 1, :]
                own[j * BB : (j + 1) * BB, kt * LANES : (kt + 1) * LANES] = block.astype(bf16)
        for p in range(NS):
            for q, src in enumerate((mine, other)):
                e = 2 * p + (c ^ q)
                a = pl.multiple_of(tab[base, 32 + e] * BLK, BB)
                b = pl.multiple_of(tab[base, 64 + e] * BLK + TO * BB, BB)
                to = pl.ds(pl.multiple_of(e * BB, BB), BB)
                parts = (src[p, pl.ds(a, TO * BB), :], src[p, pl.ds(b, TV * BB), :])
                for kt in range(KT):
                    far[to, kt * LANES : (kt + 1) * LANES] = tile_of(parts, kt)

    def multiply(own, far, prod):
        for kind, cols in enumerate((slice(0, KO), slice(KO, KO + KV))):
            prod[kind] = lax.dot_general(
                far[:, cols], own[:, cols], dims, preferred_element_type=f32
            ).astype(bf16)

    def select(d, m, prod, out):
        base = d * 8
        for t in range(NNB):
            picked = [None, None]
            for j in range(NJ):
                at = pl.multiple_of(tab[base + j, t] * BB, BB)
                for kind in range(2):
                    row = prod[kind, pl.ds(at, BB), :]
                    picked[kind] = row if j == 0 else jnp.where(lane == j, row, picked[kind])
            for kind in range(2):
                out[m, kind * TR + t * BB : kind * TR + (t + 1) * BB, :] = picked[kind]

    for k, out in zip(jobs, outs):

        def per_two(i, carry, k=k, out=out):
            ms = (2 * i, 2 * i + 1)
            ds = [(zl ^ (2 * n + i)) * NX + (x + k) % NX for n in range(2)]
            for n in range(2):
                gather(ds[n], scratch[n], scratch[2 + n])
            for n in range(2):
                multiply(scratch[n], scratch[2 + n], scratch[4 + n])
            for n in range(2):
                select(ds[n], ms[n], scratch[4 + n], out)
            return carry

        lax.fori_loop(0, NZ // 2, per_two, 0)


def dens_call(jobs, tables, pos, mine, other, wts):
    vmem = pl.BlockSpec(memory_space=pltpu.VMEM)
    smem = pl.BlockSpec(memory_space=pltpu.SMEM)
    part = jax.ShapeDtypeStruct((NZ, 2 * TR, NJ * BB), bf16)
    return pl.pallas_call(
        functools.partial(dens_kernel, jobs),
        out_shape=(part,) * len(jobs),
        in_specs=[smem, smem, vmem, vmem, vmem],
        out_specs=(vmem,) * len(jobs),
        scratch_shapes=[
            pltpu.VMEM((NJ * BB, KO + KV), bf16),
            pltpu.VMEM((NJ * BB, KO + KV), bf16),
            pltpu.VMEM((32 * BB, KO + KV), bf16),
            pltpu.VMEM((32 * BB, KO + KV), bf16),
            pltpu.VMEM((2, 32 * BB, NJ * BB), bf16),
            pltpu.VMEM((2, 32 * BB, NJ * BB), bf16),
        ],
        compiler_params=pltpu.CompilerParams(vmem_limit_bytes=24 << 20),
        cost_estimate=pl.CostEstimate(
            flops=2 * len(jobs) * NZ * 512 * 128 * (KO + KV), bytes_accessed=6 << 20, transcendentals=0
        ),
        name="density_partials",
    )(tables, pos, mine, other, wts)


def tile_kernel(
    meta, kept, moved, blocks, own, keep, give, recv, dens, occ_exp, vir_exp, kron, acc, chi, sem
):
    load = pltpu.make_async_copy(blocks, recv, sem)
    load.start()
    dens[...] = (kept[...] + moved[...].astype(f32)).astype(bf16)
    chi[...] = jnp.zeros_like(chi)
    row = lax.broadcasted_iota(jnp.int32, (NJ * BB, BB * BB), 0)
    col = lax.broadcasted_iota(jnp.int32, (NJ * BB, BB * BB), 1)

    load.wait()

    def per_pair(j, carry):
        hot_occ = (row == j * BB + col // BB).astype(f32).astype(bf16)
        hot_vir = (row == j * BB + col % BB).astype(f32).astype(bf16)
        occ_exp[...] = jnp.dot(dens[0:TR, :], hot_occ, preferred_element_type=f32)
        vir_exp[...] = jnp.dot(dens[TR : 2 * TR, :], hot_vir, preferred_element_type=f32)
        acc[...] = jnp.zeros_like(acc)
        for t in range(NNB):
            buf = t % 2
            vir = vir_exp[t * BB : (t + 1) * BB, :].astype(bf16)
            for lam in range(BB):
                occ = jnp.broadcast_to(occ_exp[t * BB + lam : t * BB + lam + 1, :], (BB, BB * BB))
                kron[buf, lam * BB : (lam + 1) * BB, :] = occ.astype(bf16) * vir
            slot = meta[j * NNB + t]
            aux = meta[128 + j * NNB + t]
            paired = jnp.dot(recv[slot], kron[buf], preferred_element_type=f32)
            acc[aux] = acc[aux] + paired
        target = meta[240 + j]
        rows = acc[...].reshape(NAB * AB, BB * BB).astype(bf16)
        chi[target] += lax.dot_general(
            own[j], rows, (((1,), (1,)), ((), ())), preferred_element_type=f32
        )
        return carry

    lax.fori_loop(0, NJ, per_pair, 0)
    low = lax.broadcasted_iota(jnp.int32, (1, 8, 128), 2) < 64
    first = jnp.full((1, 8, 128), meta[248], jnp.int32) == 0
    for tile in range(4):
        grid = chi[:, :, tile * 128 : (tile + 1) * 128].reshape(NS, 2, 2, 8, 128)
        for side, col in enumerate((2 * tile, 2 * tile + 1)):
            packed = []
            for core in range(2):
                top, bot = grid[:, core, 0], grid[:, core, 1]
                if side == 0:
                    packed.append(jnp.where(low, top, pltpu.roll(bot, 64, 2)))
                else:
                    packed.append(jnp.where(low, pltpu.roll(top, 64, 2), bot))
            keep[:, col] = jnp.where(first, packed[0], packed[1])
            give[:, col] = jnp.where(first, packed[1], packed[0])


def shift(rows, axis, size, k):
    return lax.ppermute(rows, axis, [(i, (i + k) % size) for i in range(size)]) if k else rows


def body(
    occ_coef,
    vir_coef,
    occ_weight,
    vir_weight,
    three_center,
    pair_blocks,
    send_pairs,
    partners,
    partner_blocks,
):
    zl, x, c = lax.axis_index(ZL), lax.axis_index("x"), lax.axis_index("c")
    share = zl * NX + x
    vmem = pl.BlockSpec(memory_space=pltpu.VMEM)
    smem = pl.BlockSpec(memory_space=pltpu.SMEM)
    whole = pl.BlockSpec(memory_space=pl.ANY)
    spread_out = functools.partial(lax.all_to_all, split_axis=0, concat_axis=0, tiled=True)
    extra = (pair_blocks.T, partners, partner_blocks.transpose(2, 0, 1))
    mine = spread_out(payload_call(occ_coef, vir_coef, extra), ZX)
    flip = [(0, 1), (1, 0)]
    step = jnp.arange(NX, dtype=jnp.int32)
    to_row = step[None, :] * (2 * NX) + ((x + step)[:, None] % NX) * 2
    sends = send_pairs.reshape(-1)
    kept = three_center[sends[(to_row + c).reshape(-1)]]
    given = three_center[sends[(to_row + 1 - c).reshape(-1)]]
    given = lax.ppermute(given, "c", flip)
    blocks = (NX, NZ, AB, BB * BB)
    kept, given = kept.reshape(blocks), given.reshape(blocks)
    by_x = [shift(jnp.stack([kept[k], given[k]]), "x", NX, k) for k in range(NX)]
    by_z = jnp.stack(by_x).transpose(2, 0, 1, 3, 4).reshape(32, AB, BB * BB)
    wts = jnp.concatenate(
        [
            lax.dynamic_slice_in_dim(occ_weight, share * KO, KO),
            lax.dynamic_slice_in_dim(vir_weight, share * KV, KV),
        ]
    ).reshape(KT, LANES)
    pos = jnp.stack([zl, x, c, share]).astype(jnp.int32)
    mine, by_z, wts, pos = lax.optimization_barrier((mine, by_z, wts, pos))
    received = spread_out(by_z, ZL)
    tables = mine[:, LOCAL * BLK :, :].astype(jnp.int32).reshape(NS * 8, LANES)
    other = lax.ppermute(mine, "c", flip)
    (part2,) = dens_call((2,), tables, pos, mine, other, wts)
    part2 = shift(part2, "x", NX, 1)
    part1, part3, part0 = dens_call((1, 3, 0), tables, pos, mine, other, wts)
    part1 = (part1.astype(f32) + part2.astype(f32)).astype(bf16)
    summed = part0.astype(f32)
    summed = summed + shift(part1, "x", NX, 1).astype(f32)
    summed = summed + shift(part3, "x", NX, NX - 1).astype(f32)
    crossed = lax.ppermute(summed[2:].astype(bf16), "za", flip).astype(f32)
    kept_tiles = summed[0] + crossed[0]
    moved_tiles = lax.ppermute((summed[1] + crossed[1]).astype(bf16), "zb", flip)

    slots = partners.reshape(-1)
    lag_x = (x - slots // 2 % NX) % NX
    place = (slots // (2 * NX) * NX + lag_x) * 2 + ((slots % 2) ^ c)
    pad = jnp.zeros((32,), jnp.int32)
    far_aux = partner_blocks[:, :, 2].reshape(-1)
    meta = jnp.concatenate(
        [place, pad, far_aux, pad[:16], pair_blocks[:, 2], c.astype(jnp.int32)[None], pad[:7]]
    )
    out_half = jax.ShapeDtypeStruct((NS, 8, 8, 128), f32)
    keep, give = pl.pallas_call(
        tile_kernel,
        out_shape=(out_half, out_half),
        in_specs=[smem, vmem, vmem, whole, vmem],
        out_specs=(vmem, vmem),
        scratch_shapes=[
            pltpu.VMEM((32, AB, BB * BB), bf16),
            pltpu.VMEM((2 * TR, NJ * BB), bf16),
            pltpu.VMEM((TR, BB * BB), f32),
            pltpu.VMEM((TR, BB * BB), f32),
            pltpu.VMEM((2, BB * BB, BB * BB), bf16),
            pltpu.VMEM((NAB, AB, BB * BB), f32),
            pltpu.VMEM((NAB, AB, NAB * AB), f32),
            pltpu.SemaphoreType.DMA,
        ],
        compiler_params=pltpu.CompilerParams(vmem_limit_bytes=32 << 20),
        cost_estimate=pl.CostEstimate(
            flops=2 * 96 * 128 * 256 * 256, bytes_accessed=4 << 20, transcendentals=0
        ),
        name="chi_tiles",
    )(meta, kept_tiles, moved_tiles, received, three_center)

    pair_sum = keep + lax.ppermute(give, "c", flip)
    gathered = lax.all_to_all(
        pair_sum.astype(bf16).reshape(128, 8, 128),
        ZX + ("y", "zh"),
        split_axis=0,
        concat_axis=0,
        tiled=True,
    )
    total = jnp.sum(gathered.astype(f32), axis=0)
    return jnp.concatenate([total[:, :64], total[:, 64:]], axis=0)


def solution(mesh):
    fine = Mesh(mesh.devices.reshape(2, 2, 4, 2, 4, 2), ALL)
    return jax.shard_map(
        body,
        mesh=fine,
        in_specs=(
            P(ALL, None),
            P(ALL, None),
            P(),
            P(),
            P(ALL, None, None),
            P(ALL, None),
            P(ALL, None),
            P(ALL, None),
            P(ALL, None, None),
        ),
        out_specs=P(ZX + ("c",), ("y", "zh")),
        check_vma=False,
    )
```

```python
import functools

import jax
import jax.numpy as jnp
from jax import lax
from jax.experimental import pallas as pl
from jax.experimental.pallas import tpu as pltpu
from jax.sharding import Mesh, PartitionSpec as P

BB = 16
AB = 128
NNB = 12
NAB = 4
NJ = 8
NZ = 4
NX = 4
NS = NZ * NX
LOCAL = 6
KO = 256
KV = 640
ROWS = LOCAL * BB
TR = NNB * BB
LANES = 128
TO = KO // LANES
TV = KV // LANES
KT = TO + TV
BLK = KT * BB
PAY = LOCAL * BLK + 8
ZL = ("zb", "za")
ZX = ("zb", "za", "x")
ALL = ("zb", "za", "x", "c", "y", "zh")
f32 = jnp.float32
bf16 = jnp.bfloat16


def table_of(ids, slots, far_ids):
    lane = lax.broadcasted_iota(jnp.int32, (NJ, LANES), 1)
    diag = lax.broadcasted_iota(jnp.int32, (NJ, NJ), 0) == lax.broadcasted_iota(jnp.int32, (NJ, NJ), 1)
    slot = slots[...]

    def local(block):
        return block - LOCAL * jnp.floor((block.astype(f32) + 0.5) * (1.0 / LOCAL)).astype(jnp.int32)

    own = local(ids[...])
    far_occ, far_vir = local(far_ids[0]), local(far_ids[1])
    rows = jnp.zeros((NJ, LANES), jnp.int32)
    for kind in range(2):
        column = jnp.sum(jnp.where(diag, own[kind : kind + 1, :], 0), axis=1, keepdims=True)
        rows = jnp.where(lane == 16 + kind, column, rows)
    seen = jnp.zeros((NJ, LANES), jnp.int32)
    for t in range(NNB):
        here = slot[:, t : t + 1]
        rows = jnp.where(lane == t, here, rows)
        seen = jnp.where(lane == here + 32, jnp.maximum(seen, far_occ[:, t : t + 1]), seen)
        seen = jnp.where(lane == here + 64, jnp.maximum(seen, far_vir[:, t : t + 1]), seen)
    rows = rows + jnp.max(seen, axis=0, keepdims=True)
    return rows.astype(f32).astype(bf16)


def payload_kernel(occ, vir, *refs):
    given, (out, occ_in, vir_in, packed, *small, sems_in, sems_out) = refs[:3], refs[3:]
    copies = [pltpu.make_async_copy(given[n], small[n], sems_in.at[NS, n]) for n in range(3)]
    for copy in copies:
        copy.start()
    loads, stores = [], []
    for s in range(NS):
        loads.append(
            (
                pltpu.make_async_copy(occ.at[:, pl.ds(s * KO, KO)], occ_in.at[s], sems_in.at[s, 0]),
                pltpu.make_async_copy(vir.at[:, pl.ds(s * KV, KV)], vir_in.at[s], sems_in.at[s, 1]),
            )
        )
        for load in loads[-1]:
            load.start()
    for copy in copies:
        copy.wait()
    table = table_of(*small)
    for s in range(NS):
        for load in loads[s]:
            load.wait()
        for blk in range(LOCAL):
            rows = slice(blk * BB, (blk + 1) * BB)
            for kt in range(KT):
                at = blk * BLK + kt * BB
                stage, first = (occ_in, kt) if kt < TO else (vir_in, kt - TO)
                packed[s, at : at + BB, :] = stage[s, rows, first * LANES : (first + 1) * LANES]
        packed[s, LOCAL * BLK : PAY, :] = table
        stores.append(pltpu.make_async_copy(packed.at[s], out.at[s], sems_out.at[s]))
        stores[-1].start()
    for store in stores:
        store.wait()


def payload_call(occ_coef, vir_coef, extra):
    hbm = pl.BlockSpec(memory_space=pltpu.HBM)
    return pl.pallas_call(
        payload_kernel,
        out_shape=jax.ShapeDtypeStruct((NS, PAY, LANES), bf16),
        in_specs=[hbm] * 5,
        out_specs=hbm,
        scratch_shapes=[
            pltpu.VMEM((NS, ROWS, KO), bf16),
            pltpu.VMEM((NS, ROWS, KV), bf16),
            pltpu.VMEM((NS, PAY, LANES), bf16),
        ]
        + [pltpu.VMEM(part.shape, part.dtype) for part in extra]
        + [pltpu.SemaphoreType.DMA((NS + 1, 3)), pltpu.SemaphoreType.DMA((NS,))],
        compiler_params=pltpu.CompilerParams(vmem_limit_bytes=60 << 20),
        cost_estimate=pl.CostEstimate(flops=0, bytes_accessed=6 << 20, transcendentals=0),
        name="coef_payload",
    )(occ_coef, vir_coef, *extra)


def tile_of(parts, kt):
    return parts[0][kt * BB : (kt + 1) * BB] if kt < TO else parts[1][(kt - TO) * BB : (kt - TO + 1) * BB]


def dens_kernel(jobs, tab, pos, mine, other, wts, *refs):
    outs, scratch = refs[: len(jobs)], refs[len(jobs) :]
    zl, x, c = pos[0], pos[1], pos[2]
    lane = lax.broadcasted_iota(jnp.int32, (BB, NJ * BB), 1) // BB
    dims = (((1,), (1,)), ((), ()))

    def gather(d, own, far):
        base = d * 8
        for j in range(NJ):
            a = pl.multiple_of(tab[base + j, 16] * BLK, BB)
            b = pl.multiple_of(tab[base + j, 17] * BLK + TO * BB, BB)
            parts = (mine[d, pl.ds(a, TO * BB), :], mine[d, pl.ds(b, TV * BB), :])
            for kt in range(KT):
                block = tile_of(parts, kt).astype(f32) * wts[kt : kt + 1, :]
                own[j * BB : (j + 1) * BB, kt * LANES : (kt + 1) * LANES] = block.astype(bf16)
        for p in range(NS):
            for q, src in enumerate((mine, other)):
                e = 2 * p + (c ^ q)
                a = pl.multiple_of(tab[base, 32 + e] * BLK, BB)
                b = pl.multiple_of(tab[base, 64 + e] * BLK + TO * BB, BB)
                to = pl.ds(pl.multiple_of(e * BB, BB), BB)
                parts = (src[p, pl.ds(a, TO * BB), :], src[p, pl.ds(b, TV * BB), :])
                for kt in range(KT):
                    far[to, kt * LANES : (kt + 1) * LANES] = tile_of(parts, kt)

    def multiply(own, far, prod):
        for kind, cols in enumerate((slice(0, KO), slice(KO, KO + KV))):
            prod[kind] = lax.dot_general(
                far[:, cols], own[:, cols], dims, preferred_element_type=f32
            ).astype(bf16)

    def select(d, m, prod, out):
        base = d * 8
        for t in range(NNB):
            picked = [None, None]
            for j in range(NJ):
                at = pl.multiple_of(tab[base + j, t] * BB, BB)
                for kind in range(2):
                    row = prod[kind, pl.ds(at, BB), :]
                    picked[kind] = row if j == 0 else jnp.where(lane == j, row, picked[kind])
            for kind in range(2):
                out[m, kind * TR + t * BB : kind * TR + (t + 1) * BB, :] = picked[kind]

    for k, out in zip(jobs, outs):

        def per_two(i, carry, k=k, out=out):
            ms = (2 * i, 2 * i + 1)
            ds = [(zl ^ (2 * n + i)) * NX + (x + k) % NX for n in range(2)]
            for n in range(2):
                gather(ds[n], scratch[n], scratch[2 + n])
            for n in range(2):
                multiply(scratch[n], scratch[2 + n], scratch[4 + n])
            for n in range(2):
                select(ds[n], ms[n], scratch[4 + n], out)
            return carry

        lax.fori_loop(0, NZ // 2, per_two, 0)


def dens_call(jobs, tables, pos, mine, other, wts):
    vmem = pl.BlockSpec(memory_space=pltpu.VMEM)
    smem = pl.BlockSpec(memory_space=pltpu.SMEM)
    part = jax.ShapeDtypeStruct((NZ, 2 * TR, NJ * BB), bf16)
    return pl.pallas_call(
        functools.partial(dens_kernel, jobs),
        out_shape=(part,) * len(jobs),
        in_specs=[smem, smem, vmem, vmem, vmem],
        out_specs=(vmem,) * len(jobs),
        scratch_shapes=[
            pltpu.VMEM((NJ * BB, KO + KV), bf16),
            pltpu.VMEM((NJ * BB, KO + KV), bf16),
            pltpu.VMEM((32 * BB, KO + KV), bf16),
            pltpu.VMEM((32 * BB, KO + KV), bf16),
            pltpu.VMEM((2, 32 * BB, NJ * BB), bf16),
            pltpu.VMEM((2, 32 * BB, NJ * BB), bf16),
        ],
        compiler_params=pltpu.CompilerParams(vmem_limit_bytes=24 << 20),
        cost_estimate=pl.CostEstimate(
            flops=2 * len(jobs) * NZ * 512 * 128 * (KO + KV), bytes_accessed=6 << 20, transcendentals=0
        ),
        name="density_partials",
    )(tables, pos, mine, other, wts)


def tile_kernel(
    meta, kept, moved, blocks, own, keep, give, recv, dens, *refs
):
    occs, virs, krons, accs, (chi, sem) = refs[0:4], refs[4:8], refs[8:12], refs[12:16], refs[16:]
    load = pltpu.make_async_copy(blocks, recv, sem)
    load.start()
    dens[...] = (kept[...] + moved[...].astype(f32)).astype(bf16)
    chi[...] = jnp.zeros_like(chi)
    row = lax.broadcasted_iota(jnp.int32, (NJ * BB, BB * BB), 0)
    col = lax.broadcasted_iota(jnp.int32, (NJ * BB, BB * BB), 1)

    load.wait()

    def expand(j, occ_exp, vir_exp, acc):
        hot_occ = (row == j * BB + col // BB).astype(f32).astype(bf16)
        hot_vir = (row == j * BB + col % BB).astype(f32).astype(bf16)
        occ_exp[...] = jnp.dot(dens[0:TR, :], hot_occ, preferred_element_type=f32)
        vir_exp[...] = jnp.dot(dens[TR : 2 * TR, :], hot_vir, preferred_element_type=f32)
        acc[...] = jnp.zeros_like(acc)

    def add_partner(j, t, occ_exp, vir_exp, kron, acc):
        buf = t % 2
        vir = vir_exp[t * BB : (t + 1) * BB, :].astype(bf16)
        for lam in range(BB):
            occ = jnp.broadcast_to(occ_exp[t * BB + lam : t * BB + lam + 1, :], (BB, BB * BB))
            kron[buf, lam * BB : (lam + 1) * BB, :] = occ.astype(bf16) * vir
        slot = meta[j * NNB + t]
        aux = meta[128 + j * NNB + t]
        acc[aux] = acc[aux] + jnp.dot(recv[slot], kron[buf], preferred_element_type=f32)

    def finish(j, acc):
        target = meta[240 + j]
        rows = acc[...].reshape(NAB * AB, BB * BB).astype(bf16)
        chi[target] += lax.dot_general(
            own[j], rows, (((1,), (1,)), ((), ())), preferred_element_type=f32
        )

    def per_four(i, carry):
        for n in range(4):
            expand(4 * i + n, occs[n], virs[n], accs[n])
        for t in range(NNB):
            for n in range(4):
                add_partner(4 * i + n, t, occs[n], virs[n], krons[n], accs[n])
        for n in range(4):
            finish(4 * i + n, accs[n])
        return carry

    lax.fori_loop(0, NJ // 4, per_four, 0)
    low = lax.broadcasted_iota(jnp.int32, (1, 8, 128), 2) < 64
    first = jnp.full((1, 8, 128), meta[248], jnp.int32) == 0
    for tile in range(4):
        grid = chi[:, :, tile * 128 : (tile + 1) * 128].reshape(NS, 2, 2, 8, 128)
        for side, col in enumerate((2 * tile, 2 * tile + 1)):
            packed = []
            for core in range(2):
                top, bot = grid[:, core, 0], grid[:, core, 1]
                if side == 0:
                    packed.append(jnp.where(low, top, pltpu.roll(bot, 64, 2)))
                else:
                    packed.append(jnp.where(low, pltpu.roll(top, 64, 2), bot))
            keep[:, col] = jnp.where(first, packed[0], packed[1])
            give[:, col] = jnp.where(first, packed[1], packed[0])


def shift(rows, axis, size, k):
    return lax.ppermute(rows, axis, [(i, (i + k) % size) for i in range(size)]) if k else rows


def body(
    occ_coef,
    vir_coef,
    occ_weight,
    vir_weight,
    three_center,
    pair_blocks,
    send_pairs,
    partners,
    partner_blocks,
):
    zl, x, c = lax.axis_index(ZL), lax.axis_index("x"), lax.axis_index("c")
    share = zl * NX + x
    vmem = pl.BlockSpec(memory_space=pltpu.VMEM)
    smem = pl.BlockSpec(memory_space=pltpu.SMEM)
    whole = pl.BlockSpec(memory_space=pl.ANY)
    spread_out = functools.partial(lax.all_to_all, split_axis=0, concat_axis=0, tiled=True)
    extra = (pair_blocks.T, partners, partner_blocks.transpose(2, 0, 1))
    mine = spread_out(payload_call(occ_coef, vir_coef, extra), ZX)
    flip = [(0, 1), (1, 0)]
    step = jnp.arange(NX, dtype=jnp.int32)
    to_row = step[None, :] * (2 * NX) + ((x + step)[:, None] % NX) * 2
    sends = send_pairs.reshape(-1)
    kept = three_center[sends[(to_row + c).reshape(-1)]]
    given = three_center[sends[(to_row + 1 - c).reshape(-1)]]
    given = lax.ppermute(given, "c", flip)
    blocks = (NX, NZ, AB, BB * BB)
    kept, given = kept.reshape(blocks), given.reshape(blocks)
    by_x = [shift(jnp.stack([kept[k], given[k]]), "x", NX, k) for k in range(NX)]
    by_z = jnp.stack(by_x).transpose(2, 0, 1, 3, 4).reshape(32, AB, BB * BB)
    wts = jnp.concatenate(
        [
            lax.dynamic_slice_in_dim(occ_weight, share * KO, KO),
            lax.dynamic_slice_in_dim(vir_weight, share * KV, KV),
        ]
    ).reshape(KT, LANES)
    pos = jnp.stack([zl, x, c, share]).astype(jnp.int32)
    mine, by_z, wts, pos = lax.optimization_barrier((mine, by_z, wts, pos))
    received = spread_out(by_z, ZL)
    tables = mine[:, LOCAL * BLK :, :].astype(jnp.int32).reshape(NS * 8, LANES)
    other = lax.ppermute(mine, "c", flip)
    (part2,) = dens_call((2,), tables, pos, mine, other, wts)
    part2 = shift(part2, "x", NX, 1)
    part1, part3, part0 = dens_call((1, 3, 0), tables, pos, mine, other, wts)
    part1 = (part1.astype(f32) + part2.astype(f32)).astype(bf16)
    summed = part0.astype(f32)
    summed = summed + shift(part1, "x", NX, 1).astype(f32)
    summed = summed + shift(part3, "x", NX, NX - 1).astype(f32)
    crossed = lax.ppermute(summed[2:].astype(bf16), "za", flip).astype(f32)
    kept_tiles = summed[0] + crossed[0]
    moved_tiles = lax.ppermute((summed[1] + crossed[1]).astype(bf16), "zb", flip)

    slots = partners.reshape(-1)
    lag_x = (x - slots // 2 % NX) % NX
    place = (slots // (2 * NX) * NX + lag_x) * 2 + ((slots % 2) ^ c)
    pad = jnp.zeros((32,), jnp.int32)
    far_aux = partner_blocks[:, :, 2].reshape(-1)
    meta = jnp.concatenate(
        [place, pad, far_aux, pad[:16], pair_blocks[:, 2], c.astype(jnp.int32)[None], pad[:7]]
    )
    out_half = jax.ShapeDtypeStruct((NS, 8, 8, 128), f32)
    keep, give = pl.pallas_call(
        tile_kernel,
        out_shape=(out_half, out_half),
        in_specs=[smem, vmem, vmem, whole, vmem],
        out_specs=(vmem, vmem),
        scratch_shapes=[
            pltpu.VMEM((32, AB, BB * BB), bf16),
            pltpu.VMEM((2 * TR, NJ * BB), bf16),
        ]
        + [pltpu.VMEM((TR, BB * BB), f32)] * 8
        + [pltpu.VMEM((2, BB * BB, BB * BB), bf16)] * 4
        + [pltpu.VMEM((NAB, AB, BB * BB), f32)] * 4
        + [pltpu.VMEM((NAB, AB, NAB * AB), f32), pltpu.SemaphoreType.DMA],
        compiler_params=pltpu.CompilerParams(vmem_limit_bytes=32 << 20),
        cost_estimate=pl.CostEstimate(
            flops=2 * 96 * 128 * 256 * 256, bytes_accessed=4 << 20, transcendentals=0
        ),
        name="chi_tiles",
    )(meta, kept_tiles, moved_tiles, received, three_center)

    pair_sum = keep + lax.ppermute(give, "c", flip)
    gathered = lax.all_to_all(
        pair_sum.astype(bf16).reshape(128, 8, 128),
        ZX + ("y", "zh"),
        split_axis=0,
        concat_axis=0,
        tiled=True,
    )
    total = jnp.sum(gathered.astype(f32), axis=0)
    return jnp.concatenate([total[:, :64], total[:, 64:]], axis=0)


def solution(mesh):
    fine = Mesh(mesh.devices.reshape(2, 2, 4, 2, 4, 2), ALL)
    return jax.shard_map(
        body,
        mesh=fine,
        in_specs=(
            P(ALL, None),
            P(ALL, None),
            P(),
            P(),
            P(ALL, None, None),
            P(ALL, None),
            P(ALL, None),
            P(ALL, None),
            P(ALL, None, None),
        ),
        out_specs=P(ZX + ("c",), ("y", "zh")),
        check_vma=False,
    )
```

```python
import functools

import jax
import jax.numpy as jnp
from jax import lax
from jax.experimental import pallas as pl
from jax.experimental.pallas import tpu as pltpu
from jax.sharding import Mesh, PartitionSpec as P

BB = 16
AB = 128
NNB = 12
NAB = 4
NJ = 8
NZ = 4
NX = 4
NS = NZ * NX
LOCAL = 6
KO = 256
KV = 640
ROWS = LOCAL * BB
TR = NNB * BB
LANES = 128
TO = KO // LANES
TV = KV // LANES
KT = TO + TV
BLK = KT * BB
PAY = LOCAL * BLK + 8
ZL = ("zb", "za")
ZX = ("zb", "za", "x")
ALL = ("zb", "za", "x", "c", "y", "zh")
f32 = jnp.float32
bf16 = jnp.bfloat16


def table_of(ids, slots, far_ids):
    lane = lax.broadcasted_iota(jnp.int32, (NJ, LANES), 1)
    diag = lax.broadcasted_iota(jnp.int32, (NJ, NJ), 0) == lax.broadcasted_iota(jnp.int32, (NJ, NJ), 1)
    slot = slots[...]

    def local(block):
        return block - LOCAL * jnp.floor((block.astype(f32) + 0.5) * (1.0 / LOCAL)).astype(jnp.int32)

    own = local(ids[...])
    far_occ, far_vir = local(far_ids[0]), local(far_ids[1])
    rows = jnp.zeros((NJ, LANES), jnp.int32)
    for kind in range(2):
        column = jnp.sum(jnp.where(diag, own[kind : kind + 1, :], 0), axis=1, keepdims=True)
        rows = jnp.where(lane == 16 + kind, column, rows)
    seen = jnp.zeros((NJ, LANES), jnp.int32)
    for t in range(NNB):
        here = slot[:, t : t + 1]
        rows = jnp.where(lane == t, here, rows)
        seen = jnp.where(lane == here + 32, jnp.maximum(seen, far_occ[:, t : t + 1]), seen)
        seen = jnp.where(lane == here + 64, jnp.maximum(seen, far_vir[:, t : t + 1]), seen)
    rows = rows + jnp.max(seen, axis=0, keepdims=True)
    return rows.astype(f32).astype(bf16)


def payload_kernel(occ, vir, *refs):
    given, (out, occ_in, vir_in, packed, table, *small, sems_in, sems_out) = refs[:3], refs[3:]
    copies = [pltpu.make_async_copy(given[n], small[n], sems_in.at[LOCAL, n]) for n in range(3)]
    for copy in copies:
        copy.start()
    loads, stores = [], []
    for blk in range(LOCAL):
        rows = pl.ds(blk * BB, BB)
        loads.append(
            (
                pltpu.make_async_copy(occ.at[rows], occ_in.at[rows], sems_in.at[blk, 0]),
                pltpu.make_async_copy(vir.at[rows], vir_in.at[rows], sems_in.at[blk, 1]),
            )
        )
        for load in loads[-1]:
            load.start()
    for blk in range(LOCAL):
        for load in loads[blk]:
            load.wait()
        rows = slice(blk * BB, (blk + 1) * BB)
        for s in range(NS):
            for kt in range(KT):
                stage, first = (occ_in, s * TO + kt) if kt < TO else (vir_in, s * TV + kt - TO)
                tile = stage[rows, first * LANES : (first + 1) * LANES]
                packed[blk, s, kt * BB : (kt + 1) * BB, :] = tile
        place = out.at[:, pl.ds(blk * BLK, BLK)]
        stores.append(pltpu.make_async_copy(packed.at[blk], place, sems_out.at[blk]))
        stores[-1].start()
        if blk == 2:
            for copy in copies:
                copy.wait()
            table[...] = jnp.broadcast_to(table_of(*small)[None], (NS, 8, LANES))
            rest = out.at[:, pl.ds(LOCAL * BLK, 8)]
            stores.append(pltpu.make_async_copy(table, rest, sems_out.at[LOCAL]))
            stores[-1].start()
    for store in stores:
        store.wait()


def payload_call(occ_coef, vir_coef, extra):
    hbm = pl.BlockSpec(memory_space=pltpu.HBM)
    return pl.pallas_call(
        payload_kernel,
        out_shape=jax.ShapeDtypeStruct((NS, PAY, LANES), bf16),
        in_specs=[hbm] * 5,
        out_specs=hbm,
        scratch_shapes=[
            pltpu.VMEM((ROWS, NS * KO), bf16),
            pltpu.VMEM((ROWS, NS * KV), bf16),
            pltpu.VMEM((LOCAL, NS, BLK, LANES), bf16),
            pltpu.VMEM((NS, 8, LANES), bf16),
        ]
        + [pltpu.VMEM(part.shape, part.dtype) for part in extra]
        + [pltpu.SemaphoreType.DMA((LOCAL + 1, 3)), pltpu.SemaphoreType.DMA((LOCAL + 1,))],
        compiler_params=pltpu.CompilerParams(vmem_limit_bytes=60 << 20),
        cost_estimate=pl.CostEstimate(flops=0, bytes_accessed=6 << 20, transcendentals=0),
        name="coef_payload",
    )(occ_coef, vir_coef, *extra)


def tile_of(parts, kt):
    return parts[0][kt * BB : (kt + 1) * BB] if kt < TO else parts[1][(kt - TO) * BB : (kt - TO + 1) * BB]


def dens_kernel(jobs, tab, pos, mine, other, wts, *refs):
    outs, scratch = refs[: len(jobs)], refs[len(jobs) :]
    zl, x, c = pos[0], pos[1], pos[2]
    lane = lax.broadcasted_iota(jnp.int32, (BB, NJ * BB), 1) // BB
    dims = (((1,), (1,)), ((), ()))

    def gather(d, own, far):
        base = d * 8
        for j in range(NJ):
            a = pl.multiple_of(tab[base + j, 16] * BLK, BB)
            b = pl.multiple_of(tab[base + j, 17] * BLK + TO * BB, BB)
            parts = (mine[d, pl.ds(a, TO * BB), :], mine[d, pl.ds(b, TV * BB), :])
            for kt in range(KT):
                block = tile_of(parts, kt).astype(f32) * wts[kt : kt + 1, :]
                own[j * BB : (j + 1) * BB, kt * LANES : (kt + 1) * LANES] = block.astype(bf16)
        for p in range(NS):
            for q, src in enumerate((mine, other)):
                e = 2 * p + (c ^ q)
                a = pl.multiple_of(tab[base, 32 + e] * BLK, BB)
                b = pl.multiple_of(tab[base, 64 + e] * BLK + TO * BB, BB)
                to = pl.ds(pl.multiple_of(e * BB, BB), BB)
                parts = (src[p, pl.ds(a, TO * BB), :], src[p, pl.ds(b, TV * BB), :])
                for kt in range(KT):
                    far[to, kt * LANES : (kt + 1) * LANES] = tile_of(parts, kt)

    def multiply(own, far, prod):
        for kind, cols in enumerate((slice(0, KO), slice(KO, KO + KV))):
            prod[kind] = lax.dot_general(
                far[:, cols], own[:, cols], dims, preferred_element_type=f32
            ).astype(bf16)

    def select(d, m, prod, out):
        base = d * 8
        for t in range(NNB):
            picked = [None, None]
            for j in range(NJ):
                at = pl.multiple_of(tab[base + j, t] * BB, BB)
                for kind in range(2):
                    row = prod[kind, pl.ds(at, BB), :]
                    picked[kind] = row if j == 0 else jnp.where(lane == j, row, picked[kind])
            for kind in range(2):
                out[m, kind * TR + t * BB : kind * TR + (t + 1) * BB, :] = picked[kind]

    for k, out in zip(jobs, outs):

        def per_two(i, carry, k=k, out=out):
            ms = (2 * i, 2 * i + 1)
            ds = [(zl ^ (2 * n + i)) * NX + (x + k) % NX for n in range(2)]
            for n in range(2):
                gather(ds[n], scratch[n], scratch[2 + n])
            for n in range(2):
                multiply(scratch[n], scratch[2 + n], scratch[4 + n])
            for n in range(2):
                select(ds[n], ms[n], scratch[4 + n], out)
            return carry

        lax.fori_loop(0, NZ // 2, per_two, 0)


def dens_call(jobs, tables, pos, mine, other, wts):
    vmem = pl.BlockSpec(memory_space=pltpu.VMEM)
    smem = pl.BlockSpec(memory_space=pltpu.SMEM)
    part = jax.ShapeDtypeStruct((NZ, 2 * TR, NJ * BB), bf16)
    return pl.pallas_call(
        functools.partial(dens_kernel, jobs),
        out_shape=(part,) * len(jobs),
        in_specs=[smem, smem, vmem, vmem, vmem],
        out_specs=(vmem,) * len(jobs),
        scratch_shapes=[
            pltpu.VMEM((NJ * BB, KO + KV), bf16),
            pltpu.VMEM((NJ * BB, KO + KV), bf16),
            pltpu.VMEM((32 * BB, KO + KV), bf16),
            pltpu.VMEM((32 * BB, KO + KV), bf16),
            pltpu.VMEM((2, 32 * BB, NJ * BB), bf16),
            pltpu.VMEM((2, 32 * BB, NJ * BB), bf16),
        ],
        compiler_params=pltpu.CompilerParams(vmem_limit_bytes=24 << 20),
        cost_estimate=pl.CostEstimate(
            flops=2 * len(jobs) * NZ * 512 * 128 * (KO + KV), bytes_accessed=6 << 20, transcendentals=0
        ),
        name="density_partials",
    )(tables, pos, mine, other, wts)


def tile_kernel(
    meta, kept, moved, recv, own, keep, give, dens, *refs
):
    occs, virs, krons, accs, (chi,) = refs[0:8], refs[8:16], refs[16:24], refs[24:32], refs[32:]
    dens[...] = (kept[...] + moved[...].astype(f32)).astype(bf16)
    chi[...] = jnp.zeros_like(chi)
    row = lax.broadcasted_iota(jnp.int32, (NJ * BB, BB * BB), 0)
    col = lax.broadcasted_iota(jnp.int32, (NJ * BB, BB * BB), 1)

    def expand(j, occ_exp, vir_exp, acc):
        hot_occ = (row == j * BB + col // BB).astype(f32).astype(bf16)
        hot_vir = (row == j * BB + col % BB).astype(f32).astype(bf16)
        occ_exp[...] = jnp.dot(dens[0:TR, :], hot_occ, preferred_element_type=f32)
        vir_exp[...] = jnp.dot(dens[TR : 2 * TR, :], hot_vir, preferred_element_type=f32)
        acc[...] = jnp.zeros_like(acc)

    def add_partner(j, t, occ_exp, vir_exp, kron, acc):
        buf = t % 2
        vir = vir_exp[t * BB : (t + 1) * BB, :].astype(bf16)
        for lam in range(BB):
            occ = jnp.broadcast_to(occ_exp[t * BB + lam : t * BB + lam + 1, :], (BB, BB * BB))
            kron[buf, lam * BB : (lam + 1) * BB, :] = occ.astype(bf16) * vir
        slot = meta[j * NNB + t]
        aux = meta[128 + j * NNB + t]
        acc[aux] = acc[aux] + jnp.dot(recv[slot], kron[buf], preferred_element_type=f32)

    def finish(j, acc):
        target = meta[240 + j]
        rows = acc[...].reshape(NAB * AB, BB * BB).astype(bf16)
        chi[target] += lax.dot_general(
            own[j], rows, (((1,), (1,)), ((), ())), preferred_element_type=f32
        )

    def per_all(i, carry):
        for n in range(8):
            expand(8 * i + n, occs[n], virs[n], accs[n])
        for t in range(NNB):
            for n in range(8):
                add_partner(8 * i + n, t, occs[n], virs[n], krons[n], accs[n])
        for n in range(8):
            finish(8 * i + n, accs[n])
        return carry

    lax.fori_loop(0, NJ // 8, per_all, 0)
    low = lax.broadcasted_iota(jnp.int32, (1, 8, 128), 2) < 64
    first = jnp.full((1, 8, 128), meta[248], jnp.int32) == 0
    for tile in range(4):
        grid = chi[:, :, tile * 128 : (tile + 1) * 128].reshape(NS, 2, 2, 8, 128)
        for side, col in enumerate((2 * tile, 2 * tile + 1)):
            packed = []
            for core in range(2):
                top, bot = grid[:, core, 0], grid[:, core, 1]
                if side == 0:
                    packed.append(jnp.where(low, top, pltpu.roll(bot, 64, 2)))
                else:
                    packed.append(jnp.where(low, pltpu.roll(top, 64, 2), bot))
            keep[:, col] = jnp.where(first, packed[0], packed[1])
            give[:, col] = jnp.where(first, packed[1], packed[0])


def shift(rows, axis, size, k):
    return lax.ppermute(rows, axis, [(i, (i + k) % size) for i in range(size)]) if k else rows


def body(
    occ_coef,
    vir_coef,
    occ_weight,
    vir_weight,
    three_center,
    pair_blocks,
    send_pairs,
    partners,
    partner_blocks,
):
    zl, x, c = lax.axis_index(ZL), lax.axis_index("x"), lax.axis_index("c")
    share = zl * NX + x
    vmem = pl.BlockSpec(memory_space=pltpu.VMEM)
    smem = pl.BlockSpec(memory_space=pltpu.SMEM)
    spread_out = functools.partial(lax.all_to_all, split_axis=0, concat_axis=0, tiled=True)
    extra = (pair_blocks.T, partners, partner_blocks.transpose(2, 0, 1))
    mine = spread_out(payload_call(occ_coef, vir_coef, extra), ZX)
    flip = [(0, 1), (1, 0)]
    step = jnp.arange(NX, dtype=jnp.int32)
    to_row = step[None, :] * (2 * NX) + ((x + step)[:, None] % NX) * 2
    sends = send_pairs.reshape(-1)
    kept = three_center[sends[(to_row + c).reshape(-1)]]
    given = three_center[sends[(to_row + 1 - c).reshape(-1)]]
    given = lax.ppermute(given, "c", flip)
    blocks = (NX, NZ, AB, BB * BB)
    kept, given = kept.reshape(blocks), given.reshape(blocks)
    by_x = [shift(jnp.stack([kept[k], given[k]]), "x", NX, k) for k in range(NX)]
    by_z = jnp.stack(by_x).transpose(2, 0, 1, 3, 4).reshape(32, AB, BB * BB)
    wts = jnp.concatenate(
        [
            lax.dynamic_slice_in_dim(occ_weight, share * KO, KO),
            lax.dynamic_slice_in_dim(vir_weight, share * KV, KV),
        ]
    ).reshape(KT, LANES)
    pos = jnp.stack([zl, x, c, share]).astype(jnp.int32)
    mine, by_z, wts, pos = lax.optimization_barrier((mine, by_z, wts, pos))
    received = spread_out(by_z, ZL)
    tables = mine[:, LOCAL * BLK :, :].astype(jnp.int32).reshape(NS * 8, LANES)
    other = lax.ppermute(mine, "c", flip)
    (part2,) = dens_call((2,), tables, pos, mine, other, wts)
    part2 = shift(part2, "x", NX, 1)
    part1, part3, part0 = dens_call((1, 3, 0), tables, pos, mine, other, wts)
    part1 = (part1.astype(f32) + part2.astype(f32)).astype(bf16)
    summed = part0.astype(f32)
    summed = summed + shift(part1, "x", NX, 1).astype(f32)
    summed = summed + shift(part3, "x", NX, NX - 1).astype(f32)
    crossed = lax.ppermute(summed[2:].astype(bf16), "za", flip).astype(f32)
    kept_tiles = summed[0] + crossed[0]
    moved_tiles = lax.ppermute((summed[1] + crossed[1]).astype(bf16), "zb", flip)

    slots = partners.reshape(-1)
    lag_x = (x - slots // 2 % NX) % NX
    place = (slots // (2 * NX) * NX + lag_x) * 2 + ((slots % 2) ^ c)
    pad = jnp.zeros((32,), jnp.int32)
    far_aux = partner_blocks[:, :, 2].reshape(-1)
    meta = jnp.concatenate(
        [place, pad, far_aux, pad[:16], pair_blocks[:, 2], c.astype(jnp.int32)[None], pad[:7]]
    )
    out_half = jax.ShapeDtypeStruct((NS, 8, 8, 128), f32)
    keep, give = pl.pallas_call(
        tile_kernel,
        out_shape=(out_half, out_half),
        in_specs=[smem, vmem, vmem, vmem, vmem],
        out_specs=(vmem, vmem),
        scratch_shapes=[
            pltpu.VMEM((2 * TR, NJ * BB), bf16),
        ]
        + [pltpu.VMEM((TR, BB * BB), f32)] * 16
        + [pltpu.VMEM((2, BB * BB, BB * BB), bf16)] * 8
        + [pltpu.VMEM((NAB, AB, BB * BB), f32)] * 8
        + [pltpu.VMEM((NAB, AB, NAB * AB), f32)],
        compiler_params=pltpu.CompilerParams(vmem_limit_bytes=32 << 20),
        cost_estimate=pl.CostEstimate(
            flops=2 * 96 * 128 * 256 * 256, bytes_accessed=4 << 20, transcendentals=0
        ),
        name="chi_tiles",
    )(meta, kept_tiles, moved_tiles, received, three_center)

    pair_sum = keep + lax.ppermute(give, "c", flip)
    gathered = lax.all_to_all(
        pair_sum.astype(bf16).reshape(128, 8, 128),
        ZX + ("y", "zh"),
        split_axis=0,
        concat_axis=0,
        tiled=True,
    )
    total = jnp.sum(gathered.astype(f32), axis=0)
    return jnp.concatenate([total[:, :64], total[:, 64:]], axis=0)


def solution(mesh):
    fine = Mesh(mesh.devices.reshape(2, 2, 4, 2, 4, 2), ALL)
    return jax.shard_map(
        body,
        mesh=fine,
        in_specs=(
            P(ALL, None),
            P(ALL, None),
            P(),
            P(),
            P(ALL, None, None),
            P(ALL, None),
            P(ALL, None),
            P(ALL, None),
            P(ALL, None, None),
        ),
        out_specs=P(ZX + ("c",), ("y", "zh")),
        check_vma=False,
    )
```
